32 devices in a mesh: row: 4 (over x, core), col: 8 (over z, y).
Axes of the slice: x: 2, y: 2, z: 4, core: 2. Of those that a mesh axis runs over, the one named last changes fastest.
Arguments:
- resid_tiles: bfloat16 [4, 176, 256, 256], P('row', 'col'), may hold values from -6 to 6
- tile_rows: int32 [4, 176], P('row', 'col'), may hold values from 0 to 3
- tile_owner: int32 [4, 176], P('row', 'col'), may hold values from 0 to 3
- tile_count: int32 [4, 8], P('row', 'col'), may hold values from 5 to 22
- block_pick: int32 [4, 8, 4], P(None, 'col', 'row'), may hold values from 0 to 3
- basis: float32 [32768, 512], P(('col', 'row')), may hold values from -0.0546875 to 0.0546875
Outputs:
- product_t: float32 [512, 4096], P('col', 'row')
The draws below stay inside these ranges and needn't reach their ends.
All inputs are finite; a program needn't handle non-finite values.
Results may differ from the reference program's by a relative error of at most 0.0065.
Values may be sent and summed in bfloat16 or wider, within the bound.
A program may use at most 64 MiB of HBM per device.

```python
import jax
import jax.numpy as jnp
from jax import lax

B = 256
RANK = 512
QB_DEV = 4
TILES_DEV = 22
RB_DEV = 4
ORDER = 32768
N_ROW = 4
N_COL = 8


def touch_ends(values, own_key, low, top_value):
    dims = values.shape
    spot = [jax.random.randint(jax.random.fold_in(own_key, axis), (), 0, dims[axis]) for axis in range(len(dims))]
    values = values.at[tuple(spot)].set(low)
    longest = dims.index(max(dims))
    spot[longest] = (spot[longest] + 1) % dims[longest]
    return values.at[tuple(spot)].set(top_value)


def steps_of(own_key, shape, split, smallest, high):
    def one(position, blocks):
        steps = jax.random.uniform(jax.random.fold_in(jax.random.fold_in(own_key, 6), position), (blocks,), jnp.float32, smallest / len(split), high / len(split))
        return jnp.repeat(jnp.exp(steps), shape[position] // blocks).reshape((-1,) + (1,) * (len(shape) - position - 1))

    gain = one(*split[0])
    for cut in split[1:]:
        gain = gain * one(*cut)
    return gain


def bell_draw(rng, extent, width, limit, pieces=(), kind=jnp.bfloat16):
    values = width * jax.random.normal(rng, extent, jnp.float32)
    if pieces:
        values = values * steps_of(rng, extent, pieces, -0.22, 0.18)
    return jnp.clip(values, -limit, limit).astype(kind)


def setup_inputs(seed: int = 0) -> dict:
    key_list = jax.random.split(jax.random.key(seed), 7)
    resid_tiles = bell_draw(key_list[0], (N_ROW, N_COL * TILES_DEV, B, B), 1.0, 6.0, ((0, 4), (1, 8)))
    tile_rows = touch_ends(jax.random.randint(key_list[1], (N_ROW, N_COL * TILES_DEV), 0, RB_DEV), jax.random.fold_in(key_list[1], 1), 0, RB_DEV - 1).astype(jnp.int32)
    tile_owner = touch_ends(jax.random.randint(key_list[2], (N_ROW, N_COL * TILES_DEV), 0, N_ROW), jax.random.fold_in(key_list[2], 1), 0, N_ROW - 1).astype(jnp.int32)
    tile_count = touch_ends(jax.random.randint(key_list[3], (N_ROW, N_COL), max(1, TILES_DEV // 4), TILES_DEV + 1), jax.random.fold_in(key_list[3], 1), max(1, TILES_DEV // 4), TILES_DEV).astype(jnp.int32)
    block_pick = touch_ends(jax.random.randint(key_list[4], (N_ROW, N_COL, N_ROW), 0, QB_DEV), jax.random.fold_in(key_list[4], 1), 0, QB_DEV - 1).astype(jnp.int32)
    basis = bell_draw(key_list[5], (ORDER, RANK), (TILES_DEV * N_COL * B // RB_DEV) ** -0.5, 0.0546875, ((0, 32),), jnp.float32)
    return dict(resid_tiles=resid_tiles, tile_rows=tile_rows, tile_owner=tile_owner, tile_count=tile_count, block_pick=block_pick, basis=basis)


def reference(resid_tiles, tile_rows, tile_owner, tile_count, block_pick, basis):
    blocks = basis.astype(jnp.bfloat16).reshape(N_COL, N_ROW, QB_DEV, B, RANK)

    def one_group(items):
        tiles, rows, owners, count, picks = items
        tiles = tiles.reshape(N_COL, TILES_DEV, B, B)
        rows = rows.reshape(N_COL, TILES_DEV)
        owners = owners.reshape(N_COL, TILES_DEV)

        def one_col(acc, col_items):
            col_tiles, col_rows, col_owners, col_count, col_picks, col_blocks = col_items
            chosen = col_blocks[col_owners, col_picks[col_owners]]
            prods = jnp.einsum('tab,tbk->tka', col_tiles.astype(jnp.float32), chosen.astype(jnp.float32))
            live = jnp.arange(TILES_DEV) < col_count
            row_hot = ((col_rows[:, None] == jnp.arange(RB_DEV)[None, :]) & live[:, None]).astype(jnp.float32)
            return acc + jnp.einsum('tka,ti->kia', prods, row_hot), None

        start = jnp.zeros((RANK, RB_DEV, B), jnp.float32)
        acc, unused = lax.scan(one_col, start, (tiles, rows, owners, count, picks, blocks))
        return acc.reshape(RANK, RB_DEV * B)

    parts = lax.map(one_group, (resid_tiles, tile_rows, tile_owner, tile_count, block_pick))
    return jnp.transpose(parts, (1, 0, 2)).reshape(RANK, N_ROW * RB_DEV * B)
```

```python
import functools

import jax
import jax.numpy as jnp
from jax import lax
from jax.experimental import pallas as pl
from jax.experimental.pallas import tpu as pltpu
from jax.sharding import PartitionSpec as P

RB_DEV = 4
STEPS = 4
HALVES = 2
MESH = pl.DeviceIdType.MESH


def flip(index):
    return index + 1 - 2 * lax.rem(index, 2)


def far_first(step, home):
    if step == 0:
        return lax.rem(home + 2, STEPS)
    if step == 1:
        return STEPS - 1 - home
    if step == 2:
        return flip(home)
    return home


def kernel(
    n_row,
    n_col,
    rows_ref,
    owners_ref,
    count_ref,
    picks_ref,
    tiles_hbm,
    basis_hbm,
    out_ref,
    tiles_v,
    basis_v0,
    basis_v1,
    basis_v2,
    basis_v3,
    x_send,
    x_recv,
    runs,
    sums,
    prods,
    lo_send,
    lo_recv,
    hi_send,
    hi_recv,
    prev_s,
    last_s,
    tiles_sem,
    basis_sem,
    x_send_sem,
    x_recv_sem,
    lo_send_sem,
    lo_recv_sem,
    hi_send_sem,
    hi_recv_sem,
):
    basis_v = (basis_v0, basis_v1, basis_v2, basis_v3)
    num_tiles, width, _ = tiles_v.shape
    lanes = basis_v0.shape[2]
    group = n_col // STEPS
    pairs = RB_DEV * n_row
    row = lax.axis_index("row")
    col = lax.axis_index("col")
    home = col // group
    place = lax.rem(col, group)

    chunks = [far_first(step, home) for step in range(STEPS)]
    row_peers = []
    for j in range(n_row // 2 - 1, 0, -1):
        peer = lax.rem(row + 2 * j, n_row)
        row_peers += [peer, flip(peer)]
    row_peers.append(flip(row))
    hi_peers = [flip(home), STEPS - 1 - home, flip(home)]
    lo_peers = [lax.rem(place + j, group) for j in range(1, group)]

    basis_copies = []
    for step in range(STEPS):
        cols = pl.ds(pl.multiple_of(chunks[step] * lanes, lanes), lanes)
        copy = pltpu.make_async_copy(basis_hbm.at[:, :, cols], basis_v[step], basis_sem.at[step])
        copy.start()
        basis_copies.append(copy)
    tiles_copy = pltpu.make_async_copy(tiles_hbm, tiles_v, tiles_sem)
    tiles_copy.start()

    barrier = pltpu.get_barrier_semaphore()
    greeted = [(peer, col) for peer in row_peers]
    greeted += [(row, home * group + peer) for peer in lo_peers]
    greeted += [(row, peer * group + place) for peer in hi_peers[:2]]
    for peer in greeted:
        pl.semaphore_signal(barrier, inc=1, device_id=peer, device_id_type=MESH)

    def block_of(step, peer):
        return jnp.transpose(basis_v[step][picks_ref[0, peer]]).astype(jnp.bfloat16)

    x_copies = []

    def send(step, peer):
        copy = pltpu.make_async_remote_copy(
            src_ref=x_send.at[step, peer],
            dst_ref=x_recv.at[step, row],
            send_sem=x_send_sem.at[step, peer],
            recv_sem=x_recv_sem.at[step, row],
            device_id=(peer, col),
            device_id_type=MESH,
        )
        copy.start()
        x_copies.append(copy)

    basis_copies[0].wait()
    for peer in row_peers:
        x_send[0, peer] = block_of(0, peer)
    pl.semaphore_wait(barrier, len(greeted))
    for peer in row_peers:
        send(0, peer)
    for step in range(1, STEPS):
        basis_copies[step].wait()
        for peer in row_peers:
            x_send[step, peer] = block_of(step, peer)
            send(step, peer)
    for step in range(STEPS):
        x_recv[step, row] = block_of(step, row)

    count = count_ref[0, 0]

    def link(t, last):
        key = jnp.where(t < count, rows_ref[0, t] * n_row + owners_ref[0, t], pairs)
        before = jnp.int32(num_tiles)
        new = []
        for p in range(pairs):
            before = jnp.where(key == p, last[p], before)
            new.append(jnp.where(key == p, t, last[p]))
        prev_s[t] = before
        return tuple(new)

    last = lax.fori_loop(0, num_tiles, link, (jnp.int32(num_tiles),) * pairs)
    for p in range(pairs):
        last_s[p] = last[p]

    runs[num_tiles] = jnp.zeros((width, width), jnp.float32)
    tiles_copy.wait()

    def run(t, carry):
        runs[t] = tiles_v[t].astype(jnp.float32) + runs[prev_s[t]]
        return carry

    lax.fori_loop(0, num_tiles, run, 0)

    def take(p, carry):
        sums[p] = runs[last_s[p]].astype(jnp.bfloat16)
        return carry

    lax.fori_loop(0, pairs, take, 0)

    piece = prods.shape[3]
    span = RB_DEV // HALVES
    lo_copies = []
    hi_copies = []

    def lo_copy(step, half, peer, slot):
        return pltpu.make_async_remote_copy(
            src_ref=lo_send.at[step, half, peer],
            dst_ref=lo_recv.at[step, half, slot],
            send_sem=lo_send_sem.at[step, half, peer],
            recv_sem=lo_recv_sem.at[step, half, slot],
            device_id=(row, home * group + peer),
            device_id_type=MESH,
        )

    def multiply(step):
        for peer in row_peers:
            pltpu.make_async_remote_copy(
                src_ref=x_send.at[step, peer],
                dst_ref=x_recv.at[step, peer],
                send_sem=x_send_sem.at[step, peer],
                recv_sem=x_recv_sem.at[step, peer],
                device_id=(peer, col),
                device_id_type=MESH,
            ).wait_recv()
        for half in range(HALVES):
            for i in range(span):
                total = None
                for o in range(n_row):
                    term = lax.dot_general(
                        x_recv[step, o],
                        sums[(half * span + i) * n_row + o],
                        (((1,), (1,)), ((), ())),
                        preferred_element_type=jnp.float32,
                    )
                    total = term if total is None else total + term
                prods[step, half, :, :, i * width : (i + 1) * width] = total.reshape(group, piece, width)
            for peer in lo_peers:
                lo_send[step, half, peer] = prods[step, half, peer].astype(jnp.bfloat16)
                copy = lo_copy(step, half, peer, place)
                copy.start()
                lo_copies.append(copy)

    def near_sum(step, half):
        total = prods[step, half, place]
        for peer in lo_peers:
            lo_copy(step, half, peer, peer).wait_recv()
            total = total + lo_recv[step, half, peer].astype(jnp.float32)
        return total

    def hear(step, half):
        hi_copies[step * HALVES + half].wait_recv()
        return hi_recv[step, half].astype(jnp.float32)

    def send_on(step):
        for half in range(HALVES):
            total = near_sum(step, half)
            if step == 1:
                total = total + hear(0, half)
            hi_send[step, half] = total.astype(jnp.bfloat16)
            copy = pltpu.make_async_remote_copy(
                src_ref=hi_send.at[step, half],
                dst_ref=hi_recv.at[step, half],
                send_sem=hi_send_sem.at[step, half],
                recv_sem=hi_recv_sem.at[step, half],
                device_id=(row, hi_peers[step] * group + place),
                device_id_type=MESH,
            )
            copy.start()
            hi_copies.append(copy)

    for step in range(STEPS):
        multiply(step)
        if step > 0:
            send_on(step - 1)
    for half in range(HALVES):
        total = near_sum(STEPS - 1, half) + hear(1, half) + hear(2, half)
        out_ref[:, half * span * width : (half + 1) * span * width] = total

    for copies in [x_copies, lo_copies, hi_copies]:
        for copy in copies:
            copy.wait_send()


def body(n_row, n_col, resid_tiles, tile_rows, tile_owner, tile_count, block_pick, basis):
    tiles = resid_tiles.reshape(resid_tiles.shape[1:])
    num_tiles, width, _ = tiles.shape
    rank = basis.shape[1]
    local_blocks = basis.reshape(-1, width, rank)
    held = local_blocks.shape[0]
    lanes = rank // STEPS
    group = n_col // STEPS
    piece = rank // n_col
    columns = RB_DEV * width
    pairs = RB_DEV * n_row
    smem = pl.BlockSpec(memory_space=pltpu.SMEM)
    hbm = pl.BlockSpec(memory_space=pl.ANY)
    dma = pltpu.SemaphoreType.DMA
    return pl.pallas_call(
        functools.partial(kernel, n_row, n_col),
        out_shape=pltpu.VMEM((piece, columns), jnp.float32),
        in_specs=[smem, smem, smem, smem, hbm, hbm],
        out_specs=pl.BlockSpec(memory_space=pltpu.VMEM),
        scratch_shapes=[
            pltpu.VMEM((num_tiles, width, width), jnp.bfloat16),
            *[pltpu.VMEM((held, width, lanes), jnp.float32)] * STEPS,
            pltpu.VMEM((STEPS, n_row, lanes, width), jnp.bfloat16),
            pltpu.VMEM((STEPS, n_row, lanes, width), jnp.bfloat16),
            pltpu.VMEM((num_tiles + 1, width, width), jnp.float32),
            pltpu.VMEM((pairs, width, width), jnp.bfloat16),
            pltpu.VMEM((STEPS, HALVES, group, piece, columns // HALVES), jnp.float32),
            pltpu.VMEM((STEPS, HALVES, group, piece, columns // HALVES), jnp.bfloat16),
            pltpu.VMEM((STEPS, HALVES, group, piece, columns // HALVES), jnp.bfloat16),
            pltpu.VMEM((STEPS - 1, HALVES, piece, columns // HALVES), jnp.bfloat16),
            pltpu.VMEM((STEPS - 1, HALVES, piece, columns // HALVES), jnp.bfloat16),
            pltpu.SMEM((num_tiles,), jnp.int32),
            pltpu.SMEM((pairs,), jnp.int32),
            dma,
            dma((STEPS,)),
            dma((STEPS, n_row)),
            dma((STEPS, n_row)),
            dma((STEPS, HALVES, group)),
            dma((STEPS, HALVES, group)),
            dma((STEPS - 1, HALVES)),
            dma((STEPS - 1, HALVES)),
        ],
        compiler_params=pltpu.CompilerParams(
            collective_id=0, has_side_effects=True, vmem_limit_bytes=63 << 20
        ),
    )(tile_rows, tile_owner, tile_count, block_pick.reshape(1, n_row), tiles, local_blocks)


def solution(mesh):
    in_specs = (
        P("row", "col", None, None),
        P("row", "col"),
        P("row", "col"),
        P("row", "col"),
        P(None, "col", "row"),
        P(("col", "row"), None),
    )
    return jax.shard_map(
        functools.partial(body, mesh.shape["row"], mesh.shape["col"]),
        mesh=mesh,
        in_specs=in_specs,
        out_specs=P("col", "row"),
        check_vma=False,
    )
```

```python
import functools

import jax
import jax.numpy as jnp
from jax import lax
from jax.experimental import pallas as pl
from jax.experimental.pallas import tpu as pltpu
from jax.sharding import PartitionSpec as P

RB_DEV = 4
STEPS = 4
PARTS = 4
ORDER = ((0, 1), (1, 0), (1, 1), (2, 0), (2, 1), (3, 0), (3, 1))
MESH = pl.DeviceIdType.MESH


def flip(index):
    return index + 1 - 2 * lax.rem(index, 2)


def is_inner(home):
    return (home > 0) & (home < STEPS - 1)


def targets(home):
    inner = is_inner(home)
    far = jnp.where(home < STEPS // 2, STEPS - 1, 0)
    return [
        jnp.where(inner, STEPS - 1 - far, far),
        jnp.where(inner, far, lax.rem(home + 2, STEPS)),
        jnp.where(inner, STEPS - 1 - home, flip(home)),
        home,
    ]


def receivers(home):
    return [jnp.where(is_inner(home), target, flip(home)) for target in targets(home)[:-1]]


def units_of(piece):
    cut = piece // 2 if piece % 32 == 0 else piece
    units = [(0, 0, low, cut) for low in range(0, piece, cut)]
    units += [(step, side, 0, piece) for step, side in ORDER]
    return units


def kernel(
    n_row,
    n_col,
    rows_hbm,
    owners_hbm,
    count_hbm,
    picks_hbm,
    tiles_hbm,
    basis_hbm,
    out_ref,
    rows_s,
    owners_s,
    count_s,
    picks_s,
    tiles_v,
    basis_v0,
    basis_v1,
    basis_v2,
    basis_v3,
    x_send,
    x_recv,
    runs,
    sums,
    own,
    lo_send,
    lo_recv,
    hi_send,
    hi_recv,
    prev_s,
    last_s,
    small_sem,
    relay_sem,
    tiles_sem,
    basis_sem,
    x_send_sem,
    x_recv_sem,
    lo_send_sem,
    lo_recv_sem,
    hi_send_sem,
    hi_recv_sem,
):
    basis_v = (basis_v0, basis_v1, basis_v2, basis_v3)
    num_tiles, width, _ = tiles_v.shape
    lanes = basis_v0.shape[2]
    group = n_col // STEPS
    piece = lanes // group
    pairs = RB_DEV * n_row
    span = RB_DEV // PARTS
    row = lax.axis_index("row")
    col = lax.axis_index("col")
    home = col // group
    place = lax.rem(col, group)
    inner = is_inner(home)

    chunks = targets(home)
    units = units_of(piece)
    hi_peers = receivers(home)
    row_peers = []
    for j in range(n_row // 2 - 1, 0, -1):
        peer = lax.rem(row + 2 * j, n_row)
        row_peers += [peer, flip(peer)]
    row_peers.append(flip(row))

    small_copies = []
    for n, (src, dst) in enumerate(
        [(picks_hbm, picks_s), (rows_hbm, rows_s), (owners_hbm, owners_s), (count_hbm, count_s)]
    ):
        copy = pltpu.make_async_copy(src, dst, small_sem.at[n])
        copy.start()
        small_copies.append(copy)
    basis_copies = []
    for step in range(STEPS):
        cols = pl.ds(pl.multiple_of(chunks[step] * lanes, lanes), lanes)
        copy = pltpu.make_async_copy(basis_hbm.at[:, :, cols], basis_v[step], basis_sem.at[step])
        copy.start()
        basis_copies.append(copy)
    tiles_copy = pltpu.make_async_copy(tiles_hbm, tiles_v, tiles_sem)
    tiles_copy.start()

    barrier = pltpu.get_barrier_semaphore()
    lo_peers = [lax.rem(place + j, group) for j in range(group)]
    greeted = [(peer, col) for peer in row_peers]
    greeted += [(row, home * group + peer) for peer in lo_peers[1:]]
    for peer in greeted:
        pl.semaphore_signal(barrier, inc=1, device_id=peer, device_id_type=MESH)

    @pl.when(home > 0)
    def _():
        pl.semaphore_signal(barrier, inc=1, device_id=(row, col - group), device_id_type=MESH)

    @pl.when(home < STEPS - 1)
    def _():
        pl.semaphore_signal(barrier, inc=1, device_id=(row, col + group), device_id_type=MESH)

    def pack(step, peer, ref):
        block = jnp.transpose(basis_v[step][picks_s[0, peer]]).astype(jnp.bfloat16)
        block = block.reshape(group, piece, width)
        for q in range(group):
            slot = lax.rem(q - place + group, group)
            ref[slot] = block[q]

    x_copies = []

    def x_copy(u, peer, sender):
        step, side, low, rows = units[u]
        slots = pl.ds(1, group - 1) if side == 0 else pl.ds(0, 1)
        return pltpu.make_async_remote_copy(
            src_ref=x_send.at[step, peer, slots, pl.ds(low, rows)],
            dst_ref=x_recv.at[step, sender, slots, pl.ds(low, rows)],
            send_sem=x_send_sem.at[u, peer],
            recv_sem=x_recv_sem.at[u, sender],
            device_id=(peer, col),
            device_id_type=MESH,
        )

    def send(*us):
        for u in us:
            for peer in row_peers:
                copy = x_copy(u, peer, row)
                copy.start()
                x_copies.append(copy)

    def pack_step(step):
        basis_copies[step].wait()
        for peer in row_peers:
            pack(step, peer, x_send.at[step, peer])

    def pack_own(step):
        pack(step, row, x_recv.at[step, row])

    def link(t, last):
        key = jnp.where(t < count_s[0, 0], rows_s[0, t] * n_row + owners_s[0, t], pairs)
        before = jnp.int32(num_tiles)
        new = []
        for p in range(pairs):
            before = jnp.where(key == p, last[p], before)
            new.append(jnp.where(key == p, t, last[p]))
        prev_s[t] = before
        return tuple(new)

    def run(t, carry):
        runs[t] = tiles_v[t].astype(jnp.float32) + runs[prev_s[t]]
        return carry

    def make_sums():
        for copy in small_copies[1:]:
            copy.wait()
        runs[num_tiles] = jnp.zeros((width, width), jnp.float32)
        last = (jnp.int32(num_tiles),) * pairs
        for t in range(num_tiles):
            last = link(t, last)
        for p in range(pairs):
            last_s[p] = last[p]
        tiles_copy.wait()
        lax.fori_loop(0, num_tiles, run, 0)
        for p in range(pairs):
            sums[p] = jnp.transpose(runs[last_s[p]].astype(jnp.bfloat16))

    lo_copies = []
    hi_copies = []

    def lo_copy(u, part, j):
        step, _, low, rows = units[u]
        rows = pl.ds(low, rows)
        return pltpu.make_async_remote_copy(
            src_ref=lo_send.at[step, part, j - 1, rows],
            dst_ref=lo_recv.at[step, part, group - j - 1, rows],
            send_sem=lo_send_sem.at[u, part, j - 1],
            recv_sem=lo_recv_sem.at[u, part, group - j - 1],
            device_id=(row, home * group + lo_peers[j]),
            device_id_type=MESH,
        )

    def product(u, part):
        step, side, low, rows = units[u]
        slots = range(1, group) if side == 0 else range(1)
        left = jnp.concatenate(
            [
                jnp.concatenate([x_recv[step, o, slot, low : low + rows] for slot in slots], axis=0)
                for o in range(n_row)
            ],
            axis=1,
        )
        out = []
        for i in range(part * span, (part + 1) * span):
            right = sums[i * n_row : (i + 1) * n_row].reshape(n_row * width, width)
            out.append(jnp.dot(left, right, preferred_element_type=jnp.float32))
        return jnp.concatenate(out, axis=1)

    def multiply(u):
        step, side, low, rows = units[u]
        for peer in row_peers:
            x_copy(u, peer, peer).wait_recv()
        for part in range(PARTS):
            total = product(u, part)
            if side:
                own[step, part, low : low + rows] = total
                continue
            total = total.astype(jnp.bfloat16)
            for j in range(1, group):
                lo_send[step, part, j - 1, low : low + rows] = total[(j - 1) * rows : j * rows]
                copy = lo_copy(u, part, j)
                copy.start()
                lo_copies.append(copy)

    def near_sum(step, part):
        total = own[step, part]
        for j in range(1, group):
            for u, unit in enumerate(units):
                if unit[:2] == (step, 0):
                    lo_copy(u, part, group - j).wait_recv()
            total = total + lo_recv[step, part, j - 1].astype(jnp.float32)
        return total

    def hi_copy(step, part, slot, peer):
        return pltpu.make_async_remote_copy(
            src_ref=hi_send.at[step, part],
            dst_ref=hi_recv.at[slot, part],
            send_sem=hi_send_sem.at[step, part],
            recv_sem=hi_recv_sem.at[slot, part],
            device_id=(row, peer * group + place),
            device_id_type=MESH,
        )

    def hear(slot, part):
        hi_copy(0, part, slot, home).wait_recv()
        return hi_recv[slot, part].astype(jnp.float32)

    def send_on(step, *parts):
        for part in parts:
            total = near_sum(step, part)
            if step == 0:
                hi_send[step, part] = total.astype(jnp.bfloat16)
            else:

                @pl.when(inner)
                def _():
                    if (step, part) == (1, 0):
                        pl.semaphore_wait(relay_sem, 1)
                    hi_send[step, part] = (total + hear(step - 1, part)).astype(jnp.bfloat16)

                @pl.when(jnp.logical_not(inner))
                def _():
                    hi_send[step, part] = total.astype(jnp.bfloat16)

            slot = jnp.where(inner, STEPS - 1, step) if step == STEPS - 2 else step
            copy = hi_copy(step, part, slot, hi_peers[step])
            copy.start()
            hi_copies.append(copy)

    def finish(*parts):
        first_slot = jnp.where(inner, 2, 0)
        for part in parts:
            cols = slice(part * span * width, (part + 1) * span * width)
            total = near_sum(STEPS - 1, part) + hear(first_slot, part)
            out_ref[:, cols] = total + hear(first_slot + 1, part)

    small_copies[0].wait()
    pack_step(0)
    pl.semaphore_wait(barrier, len(greeted) + jnp.where(inner, 2, 1))
    first = len(units) - len(ORDER)
    send(*range(first))

    @pl.when(inner)
    def _():
        other = STEPS - 1 - home
        pl.semaphore_signal(relay_sem, inc=1, device_id=(row, other * group + place), device_id_type=MESH)

    pack_step(1)
    send(first, first + 1)
    pack_own(0)
    make_sums()
    for u in range(first):
        multiply(u)
    pack_step(2)
    send(first + 2, first + 3)
    pack_step(3)
    send(first + 4, first + 5, first + 6)
    pack_own(1)
    multiply(first)
    multiply(first + 1)
    pack_own(2)
    pack_own(3)
    send_on(0, 0, 1)
    multiply(first + 2)
    send_on(0, 2, 3)
    multiply(first + 3)
    send_on(1, 0, 1)
    multiply(first + 4)
    send_on(1, 2, 3)
    multiply(first + 5)
    send_on(2, 0, 1, 2, 3)
    multiply(first + 6)
    finish(0, 1, 2, 3)
    for copies in [x_copies, lo_copies, hi_copies]:
        for copy in copies:
            copy.wait_send()


def body(n_row, n_col, resid_tiles, tile_rows, tile_owner, tile_count, block_pick, basis):
    tiles = resid_tiles.reshape(resid_tiles.shape[1:])
    num_tiles, width, _ = tiles.shape
    rank = basis.shape[1]
    local_blocks = basis.reshape(-1, width, rank)
    held = local_blocks.shape[0]
    lanes = rank // STEPS
    group = n_col // STEPS
    piece = rank // n_col
    columns = RB_DEV * width
    part = columns // PARTS
    pairs = RB_DEV * n_row
    num_units = len(units_of(piece))
    hbm = pl.BlockSpec(memory_space=pl.ANY)
    dma = pltpu.SemaphoreType.DMA
    return pl.pallas_call(
        functools.partial(kernel, n_row, n_col),
        out_shape=pltpu.VMEM((piece, columns), jnp.float32),
        in_specs=[hbm] * 6,
        out_specs=pl.BlockSpec(memory_space=pltpu.VMEM),
        scratch_shapes=[
            pltpu.SMEM((1, num_tiles), jnp.int32),
            pltpu.SMEM((1, num_tiles), jnp.int32),
            pltpu.SMEM((1, 1), jnp.int32),
            pltpu.SMEM((1, n_row), jnp.int32),
            pltpu.VMEM((num_tiles, width, width), jnp.bfloat16),
            *[pltpu.VMEM((held, width, lanes), jnp.float32)] * STEPS,
            pltpu.VMEM((STEPS, n_row, group, piece, width), jnp.bfloat16),
            pltpu.VMEM((STEPS, n_row, group, piece, width), jnp.bfloat16),
            pltpu.VMEM((num_tiles + 1, width, width), jnp.float32),
            pltpu.VMEM((pairs, width, width), jnp.bfloat16),
            pltpu.VMEM((STEPS, PARTS, piece, part), jnp.float32),
            pltpu.VMEM((STEPS, PARTS, group - 1, piece, part), jnp.bfloat16),
            pltpu.VMEM((STEPS, PARTS, group - 1, piece, part), jnp.bfloat16),
            pltpu.VMEM((STEPS - 1, PARTS, piece, part), jnp.bfloat16),
            pltpu.VMEM((STEPS, PARTS, piece, part), jnp.bfloat16),
            pltpu.SMEM((num_tiles,), jnp.int32),
            pltpu.SMEM((pairs,), jnp.int32),
            dma((4,)),
            pltpu.SemaphoreType.REGULAR,
            dma,
            dma((STEPS,)),
            dma((num_units, n_row)),
            dma((num_units, n_row)),
            dma((num_units, PARTS, group - 1)),
            dma((num_units, PARTS, group - 1)),
            dma((STEPS - 1, PARTS)),
            dma((STEPS, PARTS)),
        ],
        compiler_params=pltpu.CompilerParams(
            collective_id=0, has_side_effects=True, vmem_limit_bytes=63 << 20
        ),
    )(tile_rows, tile_owner, tile_count, block_pick.reshape(1, n_row), tiles, local_blocks)


def solution(mesh):
    in_specs = (
        P("row", "col", None, None),
        P("row", "col"),
        P("row", "col"),
        P("row", "col"),
        P(None, "col", "row"),
        P(("col", "row"), None),
    )
    return jax.shard_map(
        functools.partial(body, mesh.shape["row"], mesh.shape["col"]),
        mesh=mesh,
        in_specs=in_specs,
        out_specs=P("col", "row"),
        check_vma=False,
    )
```

```python
import functools

import jax
import jax.numpy as jnp
from jax import lax
from jax.experimental import pallas as pl
from jax.experimental.pallas import tpu as pltpu
from jax.sharding import PartitionSpec as P

RB_DEV = 4
STEPS = 4
PARTS = 4
ORDER = ((1, 0), (0, 1), (2, 0), (1, 1), (2, 1), (3, 0), (3, 1))
MESH = pl.DeviceIdType.MESH


def flip(index):
    return index + 1 - 2 * lax.rem(index, 2)


def is_inner(home):
    return (home > 0) & (home < STEPS - 1)


def targets(home):
    inner = is_inner(home)
    far = jnp.where(home < STEPS // 2, STEPS - 1, 0)
    return [
        jnp.where(inner, STEPS - 1 - far, far),
        jnp.where(inner, far, lax.rem(home + 2, STEPS)),
        jnp.where(inner, STEPS - 1 - home, flip(home)),
        home,
    ]


def receivers(home):
    return [jnp.where(is_inner(home), target, flip(home)) for target in targets(home)[:-1]]


def units_of(piece):
    cut = 16 if piece > 16 else piece
    units = [(0, 0, 0, cut)]
    if cut < piece:
        units.append((0, 0, cut, piece - cut))
    units += [(step, side, 0, piece) for step, side in ORDER]
    return units


def kernel(
    n_row,
    n_col,
    rows_hbm,
    owners_hbm,
    count_hbm,
    picks_hbm,
    tiles_hbm,
    basis_hbm,
    out_ref,
    rows_s,
    owners_s,
    count_s,
    picks_s,
    tiles_v,
    basis_v0,
    basis_v1,
    basis_v2,
    basis_v3,
    x_send,
    x_recv,
    runs,
    sums,
    own,
    lo_send,
    lo_recv,
    hi_send,
    hi_recv,
    prev_s,
    last_s,
    small_sem,
    relay_sem,
    tiles_sem,
    basis_sem,
    x_send_sem,
    x_recv_sem,
    twin_send_sem,
    twin_recv_sem,
    lo_send_sem,
    lo_recv_sem,
    hi_send_sem,
    hi_recv_sem,
):
    basis_v = (basis_v0, basis_v1, basis_v2, basis_v3)
    num_tiles, width, _ = tiles_v.shape
    lanes = basis_v0.shape[2]
    group = n_col // STEPS
    piece = lanes // group
    pairs = RB_DEV * n_row
    span = RB_DEV // PARTS
    row = lax.axis_index("row")
    col = lax.axis_index("col")
    home = col // group
    place = lax.rem(col, group)
    inner = is_inner(home)

    chunks = targets(home)
    units = units_of(piece)
    hi_peers = receivers(home)
    twin_units = [[unit[0] for unit in units].index(step) for step in range(STEPS)]
    row_peers = []
    for j in range(n_row // 2 - 1, 0, -1):
        peer = lax.rem(row - lax.rem(row, 2) + 2 * j, n_row)
        row_peers += [peer, peer + 1]
    twin = flip(row)
    row_peers.append(twin)

    small_copies = []
    for n, (src, dst) in enumerate(
        [(picks_hbm, picks_s), (rows_hbm, rows_s), (owners_hbm, owners_s), (count_hbm, count_s)]
    ):
        copy = pltpu.make_async_copy(src, dst, small_sem.at[n])
        copy.start()
        small_copies.append(copy)
    basis_copies = []
    for step in range(STEPS):
        cols = pl.ds(pl.multiple_of(chunks[step] * lanes, lanes), lanes)
        copy = pltpu.make_async_copy(basis_hbm.at[:, :, cols], basis_v[step], basis_sem.at[step])
        copy.start()
        basis_copies.append(copy)
    tiles_copy = pltpu.make_async_copy(tiles_hbm, tiles_v, tiles_sem)
    tiles_copy.start()

    barrier = pltpu.get_barrier_semaphore()
    lo_peers = [lax.rem(place + j, group) for j in range(group)]
    greeted = [(peer, col) for peer in row_peers]
    greeted += [(row, home * group + peer) for peer in lo_peers[1:]]
    for peer in greeted:
        pl.semaphore_signal(barrier, inc=1, device_id=peer, device_id_type=MESH)

    @pl.when(home > 0)
    def _():
        pl.semaphore_signal(barrier, inc=1, device_id=(row, col - group), device_id_type=MESH)

    @pl.when(home < STEPS - 1)
    def _():
        pl.semaphore_signal(barrier, inc=1, device_id=(row, col + group), device_id_type=MESH)

    def pack(step, peer, ref):
        block = jnp.transpose(basis_v[step][picks_s[0, peer]]).astype(jnp.bfloat16)
        block = block.reshape(group, piece, width)
        for q in range(group):
            slot = lax.rem(q - place + group, group)
            ref[slot] = block[q]

    x_copies = []

    def x_copy(u, peer, sender):
        step, side, low, rows = units[u]
        slots = pl.ds(1, group - 1) if side == 0 else pl.ds(0, 1)
        return pltpu.make_async_remote_copy(
            src_ref=x_send.at[step, peer, slots, pl.ds(low, rows)],
            dst_ref=x_recv.at[step, sender, slots, pl.ds(low, rows)],
            send_sem=x_send_sem.at[u, peer],
            recv_sem=x_recv_sem.at[u, sender],
            device_id=(peer, col),
            device_id_type=MESH,
        )

    def twin_copy(step, sender):
        return pltpu.make_async_remote_copy(
            src_ref=x_send.at[step, twin],
            dst_ref=x_recv.at[step, sender],
            send_sem=twin_send_sem.at[step],
            recv_sem=twin_recv_sem.at[step],
            device_id=(twin, col),
            device_id_type=MESH,
        )

    def send_twin(*steps):
        for step in steps:
            copy = twin_copy(step, row)
            copy.start()
            x_copies.append(copy)

    def send(*us):
        for u in us:
            for peer in row_peers[:-1]:
                copy = x_copy(u, peer, row)
                copy.start()
                x_copies.append(copy)

    def pack_step(step):
        basis_copies[step].wait()
        for peer in row_peers:
            pack(step, peer, x_send.at[step, peer])

    def pack_own(step):
        pack(step, row, x_recv.at[step, row])

    def link(t, last):
        key = jnp.where(t < count_s[0, 0], rows_s[0, t] * n_row + owners_s[0, t], pairs)
        before = jnp.int32(num_tiles)
        new = []
        for p in range(pairs):
            before = jnp.where(key == p, last[p], before)
            new.append(jnp.where(key == p, t, last[p]))
        prev_s[t] = before
        return tuple(new)

    def run(t, carry):
        runs[t] = tiles_v[t].astype(jnp.float32) + runs[prev_s[t]]
        return carry

    def make_sums():
        for copy in small_copies[1:]:
            copy.wait()
        runs[num_tiles] = jnp.zeros((width, width), jnp.float32)
        last = (jnp.int32(num_tiles),) * pairs
        for t in range(num_tiles):
            last = link(t, last)
        for p in range(pairs):
            last_s[p] = last[p]
        tiles_copy.wait()
        lax.fori_loop(0, num_tiles, run, 0)
        for p in range(pairs):
            sums[p] = jnp.transpose(runs[last_s[p]].astype(jnp.bfloat16))

    lo_copies = []
    hi_copies = []

    def lo_copy(u, part, j):
        step, _, low, rows = units[u]
        rows = pl.ds(low, rows)
        return pltpu.make_async_remote_copy(
            src_ref=lo_send.at[step, part, j - 1, rows],
            dst_ref=lo_recv.at[step, part, group - j - 1, rows],
            send_sem=lo_send_sem.at[u, part, j - 1],
            recv_sem=lo_recv_sem.at[u, part, group - j - 1],
            device_id=(row, home * group + lo_peers[j]),
            device_id_type=MESH,
        )

    def product(u, part):
        step, side, low, rows = units[u]
        slots = range(1, group) if side == 0 else range(1)
        left = jnp.concatenate(
            [
                jnp.concatenate([x_recv[step, o, slot, low : low + rows] for slot in slots], axis=0)
                for o in range(n_row)
            ],
            axis=1,
        )
        out = []
        for i in range(part * span, (part + 1) * span):
            right = sums[i * n_row : (i + 1) * n_row].reshape(n_row * width, width)
            out.append(jnp.dot(left, right, preferred_element_type=jnp.float32))
        return jnp.concatenate(out, axis=1)

    def multiply(u):
        step, side, low, rows = units[u]
        if u in twin_units:
            twin_copy(step, twin).wait_recv()
        for peer in row_peers[:-1]:
            x_copy(u, peer, peer).wait_recv()
        for part in range(PARTS):
            total = product(u, part)
            if side:
                own[step, part, low : low + rows] = total
                continue
            total = total.astype(jnp.bfloat16)
            for j in range(1, group):
                lo_send[step, part, j - 1, low : low + rows] = total[(j - 1) * rows : j * rows]
                copy = lo_copy(u, part, j)
                copy.start()
                lo_copies.append(copy)

    def near_sum(step, part):
        total = own[step, part]
        for j in range(1, group):
            for u, unit in enumerate(units):
                if unit[:2] == (step, 0):
                    lo_copy(u, part, group - j).wait_recv()
            total = total + lo_recv[step, part, j - 1].astype(jnp.float32)
        return total

    def hi_copy(step, part, slot, peer):
        return pltpu.make_async_remote_copy(
            src_ref=hi_send.at[step, part],
            dst_ref=hi_recv.at[slot, part],
            send_sem=hi_send_sem.at[step, part],
            recv_sem=hi_recv_sem.at[slot, part],
            device_id=(row, peer * group + place),
            device_id_type=MESH,
        )

    def hear(slot, part):
        hi_copy(0, part, slot, home).wait_recv()
        return hi_recv[slot, part].astype(jnp.float32)

    def send_on(step, *parts):
        for part in parts:
            total = near_sum(step, part)
            if step == 0:
                hi_send[step, part] = total.astype(jnp.bfloat16)
            else:

                @pl.when(inner)
                def _():
                    if (step, part) == (1, 0):
                        pl.semaphore_wait(relay_sem, 1)
                    hi_send[step, part] = (total + hear(step - 1, part)).astype(jnp.bfloat16)

                @pl.when(jnp.logical_not(inner))
                def _():
                    hi_send[step, part] = total.astype(jnp.bfloat16)

            slot = jnp.where(inner, STEPS - 1, step) if step == STEPS - 2 else step
            copy = hi_copy(step, part, slot, hi_peers[step])
            copy.start()
            hi_copies.append(copy)

    def finish(*parts):
        first_slot = jnp.where(inner, 2, 0)
        for part in parts:
            cols = slice(part * span * width, (part + 1) * span * width)
            total = near_sum(STEPS - 1, part) + hear(first_slot, part)
            out_ref[:, cols] = total + hear(first_slot + 1, part)

    small_copies[0].wait()
    pack_step(0)
    pl.semaphore_wait(barrier, len(greeted) + jnp.where(inner, 2, 1))
    first = len(units) - len(ORDER)
    send(*range(first))

    @pl.when(inner)
    def _():
        other = STEPS - 1 - home
        pl.semaphore_signal(relay_sem, inc=1, device_id=(row, other * group + place), device_id_type=MESH)

    send_twin(0)
    pack_step(1)
    send(first, first + 1)
    send_twin(1)
    pack_own(0)
    make_sums()
    for u in range(first):
        multiply(u)
    pack_step(2)
    send(first + 2, first + 3)
    send_twin(2)
    pack_step(3)
    send(first + 4, first + 5, first + 6)
    send_twin(3)
    pack_own(1)
    multiply(first)
    multiply(first + 1)
    pack_own(2)
    pack_own(3)
    send_on(0, 0, 1, 2, 3)
    multiply(first + 2)
    multiply(first + 3)
    send_on(1, 0, 1)
    multiply(first + 4)
    send_on(1, 2, 3)
    multiply(first + 5)
    send_on(2, 0, 1, 2, 3)
    multiply(first + 6)
    finish(0, 1, 2, 3)
    for copies in [x_copies, lo_copies, hi_copies]:
        for copy in copies:
            copy.wait_send()


def body(n_row, n_col, resid_tiles, tile_rows, tile_owner, tile_count, block_pick, basis):
    tiles = resid_tiles.reshape(resid_tiles.shape[1:])
    num_tiles, width, _ = tiles.shape
    rank = basis.shape[1]
    local_blocks = basis.reshape(-1, width, rank)
    held = local_blocks.shape[0]
    lanes = rank // STEPS
    group = n_col // STEPS
    piece = rank // n_col
    columns = RB_DEV * width
    part = columns // PARTS
    pairs = RB_DEV * n_row
    num_units = len(units_of(piece))
    hbm = pl.BlockSpec(memory_space=pl.ANY)
    dma = pltpu.SemaphoreType.DMA
    return pl.pallas_call(
        functools.partial(kernel, n_row, n_col),
        out_shape=pltpu.VMEM((piece, columns), jnp.float32),
        in_specs=[hbm] * 6,
        out_specs=pl.BlockSpec(memory_space=pltpu.VMEM),
        scratch_shapes=[
            pltpu.SMEM((1, num_tiles), jnp.int32),
            pltpu.SMEM((1, num_tiles), jnp.int32),
            pltpu.SMEM((1, 1), jnp.int32),
            pltpu.SMEM((1, n_row), jnp.int32),
            pltpu.VMEM((num_tiles, width, width), jnp.bfloat16),
            *[pltpu.VMEM((held, width, lanes), jnp.float32)] * STEPS,
            pltpu.VMEM((STEPS, n_row, group, piece, width), jnp.bfloat16),
            pltpu.VMEM((STEPS, n_row, group, piece, width), jnp.bfloat16),
            pltpu.VMEM((num_tiles + 1, width, width), jnp.float32),
            pltpu.VMEM((pairs, width, width), jnp.bfloat16),
            pltpu.VMEM((STEPS, PARTS, piece, part), jnp.float32),
            pltpu.VMEM((STEPS, PARTS, group - 1, piece, part), jnp.bfloat16),
            pltpu.VMEM((STEPS, PARTS, group - 1, piece, part), jnp.bfloat16),
            pltpu.VMEM((STEPS - 1, PARTS, piece, part), jnp.bfloat16),
            pltpu.VMEM((STEPS, PARTS, piece, part), jnp.bfloat16),
            pltpu.SMEM((num_tiles,), jnp.int32),
            pltpu.SMEM((pairs,), jnp.int32),
            dma((4,)),
            pltpu.SemaphoreType.REGULAR,
            dma,
            dma((STEPS,)),
            dma((num_units, n_row)),
            dma((num_units, n_row)),
            dma((STEPS,)),
            dma((STEPS,)),
            dma((num_units, PARTS, group - 1)),
            dma((num_units, PARTS, group - 1)),
            dma((STEPS - 1, PARTS)),
            dma((STEPS, PARTS)),
        ],
        compiler_params=pltpu.CompilerParams(
            collective_id=0, has_side_effects=True, vmem_limit_bytes=63 << 20
        ),
    )(tile_rows, tile_owner, tile_count, block_pick.reshape(1, n_row), tiles, local_blocks)


def solution(mesh):
    in_specs = (
        P("row", "col", None, None),
        P("row", "col"),
        P("row", "col"),
        P("row", "col"),
        P(None, "col", "row"),
        P(("col", "row"), None),
    )
    return jax.shard_map(
        functools.partial(body, mesh.shape["row"], mesh.shape["col"]),
        mesh=mesh,
        in_specs=in_specs,
        out_specs=P("col", "row"),
        check_vma=False,
    )
```

```python
import functools

import jax
import jax.numpy as jnp
from jax import lax
from jax.experimental import pallas as pl
from jax.experimental.pallas import tpu as pltpu
from jax.sharding import PartitionSpec as P

RB_DEV = 4
STEPS = 4
PARTS = 4
ORDER = ((1, 0), (0, 1), (2, 0), (1, 1), (3, 0), (2, 1), (3, 1))
MESH = pl.DeviceIdType.MESH


def flip(index):
    return index + 1 - 2 * lax.rem(index, 2)


def is_inner(home):
    return (home > 0) & (home < STEPS - 1)


def targets(home):
    inner = is_inner(home)
    far = jnp.where(home < STEPS // 2, STEPS - 1, 0)
    return [
        jnp.where(inner, STEPS - 1 - far, far),
        jnp.where(inner, far, lax.rem(home + 2, STEPS)),
        jnp.where(inner, STEPS - 1 - home, flip(home)),
        home,
    ]


def receivers(home):
    return [jnp.where(is_inner(home), target, flip(home)) for target in targets(home)[:-1]]


def units_of(piece):
    cut = 16 if piece > 16 else piece
    units = [(0, 0, 0, cut)]
    if cut < piece:
        units.append((0, 0, cut, piece - cut))
    units += [(step, side, 0, piece) for step, side in ORDER]
    return units


def kernel(
    n_row,
    n_col,
    rows_hbm,
    owners_hbm,
    count_hbm,
    picks_hbm,
    tiles_hbm,
    basis_hbm,
    out_ref,
    rows_s,
    owners_s,
    count_s,
    picks_s,
    tiles_v,
    basis_v0,
    basis_v1,
    basis_v2,
    basis_v3,
    x_send,
    x_recv,
    runs,
    sums,
    own,
    lo_send,
    lo_recv,
    hi_send,
    hi_recv,
    prev_s,
    last_s,
    small_sem,
    relay_sem,
    tiles_sem,
    basis_sem,
    x_send_sem,
    x_recv_sem,
    twin_send_sem,
    twin_recv_sem,
    lo_send_sem,
    lo_recv_sem,
    hi_send_sem,
    hi_recv_sem,
):
    basis_v = (basis_v0, basis_v1, basis_v2, basis_v3)
    num_tiles, width, _ = tiles_v.shape
    lanes = basis_v0.shape[2]
    group = n_col // STEPS
    piece = lanes // group
    pairs = RB_DEV * n_row
    span = RB_DEV // PARTS
    row = lax.axis_index("row")
    col = lax.axis_index("col")
    home = col // group
    place = lax.rem(col, group)
    inner = is_inner(home)

    chunks = targets(home)
    units = units_of(piece)
    hi_peers = receivers(home)
    twin_units = [[unit[0] for unit in units].index(step) for step in range(STEPS)]
    row_peers = []
    for j in range(n_row // 2 - 1, 0, -1):
        peer = lax.rem(row - lax.rem(row, 2) + 2 * j, n_row)
        row_peers += [peer, peer + 1]
    twin = flip(row)
    row_peers.append(twin)

    small_copies = []
    for n, (src, dst) in enumerate(
        [(picks_hbm, picks_s), (rows_hbm, rows_s), (owners_hbm, owners_s), (count_hbm, count_s)]
    ):
        copy = pltpu.make_async_copy(src, dst, small_sem.at[n])
        copy.start()
        small_copies.append(copy)
    basis_copies = []
    for step in range(STEPS):
        cols = pl.ds(pl.multiple_of(chunks[step] * lanes, lanes), lanes)
        copy = pltpu.make_async_copy(basis_hbm.at[:, :, cols], basis_v[step], basis_sem.at[step])
        copy.start()
        basis_copies.append(copy)
    tiles_copy = pltpu.make_async_copy(tiles_hbm, tiles_v, tiles_sem)
    tiles_copy.start()

    barrier = pltpu.get_barrier_semaphore()
    lo_peers = [lax.rem(place + j, group) for j in range(group)]
    greeted = [(peer, col) for peer in row_peers]
    greeted += [(row, home * group + peer) for peer in lo_peers[1:]]
    for peer in greeted:
        pl.semaphore_signal(barrier, inc=1, device_id=peer, device_id_type=MESH)

    @pl.when(home > 0)
    def _():
        pl.semaphore_signal(barrier, inc=1, device_id=(row, col - group), device_id_type=MESH)

    @pl.when(home < STEPS - 1)
    def _():
        pl.semaphore_signal(barrier, inc=1, device_id=(row, col + group), device_id_type=MESH)

    def pack(step, peer, ref):
        block = jnp.transpose(basis_v[step][picks_s[0, peer]]).astype(jnp.bfloat16)
        block = block.reshape(group, piece, width)
        for q in range(group):
            slot = lax.rem(q - place + group, group)
            ref[slot] = block[q]

    x_copies = []

    def x_copy(u, peer, sender):
        step, side, low, rows = units[u]
        slots = pl.ds(1, group - 1) if side == 0 else pl.ds(0, 1)
        return pltpu.make_async_remote_copy(
            src_ref=x_send.at[step, peer, slots, pl.ds(low, rows)],
            dst_ref=x_recv.at[step, sender, slots, pl.ds(low, rows)],
            send_sem=x_send_sem.at[u, peer],
            recv_sem=x_recv_sem.at[u, sender],
            device_id=(peer, col),
            device_id_type=MESH,
        )

    def twin_copy(step, sender):
        return pltpu.make_async_remote_copy(
            src_ref=x_send.at[step, twin],
            dst_ref=x_recv.at[step, sender],
            send_sem=twin_send_sem.at[step],
            recv_sem=twin_recv_sem.at[step],
            device_id=(twin, col),
            device_id_type=MESH,
        )

    def send_twin(*steps):
        for step in steps:
            copy = twin_copy(step, row)
            copy.start()
            x_copies.append(copy)

    def send(*us):
        for u in us:
            for peer in row_peers[:-1]:
                copy = x_copy(u, peer, row)
                copy.start()
                x_copies.append(copy)

    def pack_step(step):
        basis_copies[step].wait()
        for peer in row_peers:
            pack(step, peer, x_send.at[step, peer])

    def pack_own(step):
        pack(step, row, x_recv.at[step, row])

    def link(t, last):
        key = jnp.where(t < count_s[0, 0], rows_s[0, t] * n_row + owners_s[0, t], pairs)
        before = jnp.int32(num_tiles)
        new = []
        for p in range(pairs):
            before = jnp.where(key == p, last[p], before)
            new.append(jnp.where(key == p, t, last[p]))
        prev_s[t] = before
        return tuple(new)

    def run(t, carry):
        runs[t] = tiles_v[t].astype(jnp.float32) + runs[prev_s[t]]
        return carry

    def make_sums():
        for copy in small_copies[1:]:
            copy.wait()
        runs[num_tiles] = jnp.zeros((width, width), jnp.float32)
        last = (jnp.int32(num_tiles),) * pairs
        for t in range(num_tiles):
            last = link(t, last)
        for p in range(pairs):
            last_s[p] = last[p]
        tiles_copy.wait()
        lax.fori_loop(0, num_tiles, run, 0)
        for p in range(pairs):
            sums[p] = jnp.transpose(runs[last_s[p]].astype(jnp.bfloat16))

    lo_copies = []
    hi_copies = []

    def lo_copy(u, part, j):
        step, _, low, rows = units[u]
        rows = pl.ds(low, rows)
        return pltpu.make_async_remote_copy(
            src_ref=lo_send.at[step, part, j - 1, rows],
            dst_ref=lo_recv.at[step, part, group - j - 1, rows],
            send_sem=lo_send_sem.at[u, part, j - 1],
            recv_sem=lo_recv_sem.at[u, part, group - j - 1],
            device_id=(row, home * group + lo_peers[j]),
            device_id_type=MESH,
        )

    def product(u, part):
        step, side, low, rows = units[u]
        slots = range(1, group) if side == 0 else range(1)
        left = jnp.concatenate(
            [
                jnp.concatenate([x_recv[step, o, slot, low : low + rows] for slot in slots], axis=0)
                for o in range(n_row)
            ],
            axis=1,
        )
        out = []
        for i in range(part * span, (part + 1) * span):
            right = sums[i * n_row : (i + 1) * n_row].reshape(n_row * width, width)
            out.append(jnp.dot(left, right, preferred_element_type=jnp.float32))
        return jnp.concatenate(out, axis=1)

    def multiply(u, between=()):
        step, side, low, rows = units[u]
        if u in twin_units:
            twin_copy(step, twin).wait_recv()
        for peer in row_peers[:-1]:
            x_copy(u, peer, peer).wait_recv()
        for part in range(PARTS):
            total = product(u, part)
            if side:
                own[step, part, low : low + rows] = total
            else:
                total = total.astype(jnp.bfloat16)
                for j in range(1, group):
                    lo_send[step, part, j - 1, low : low + rows] = total[(j - 1) * rows : j * rows]
                    copy = lo_copy(u, part, j)
                    copy.start()
                    lo_copies.append(copy)
            for after, late_step, late_part in between:
                if after == part:
                    send_on(late_step, late_part)

    def near_sum(step, part):
        total = own[step, part]
        for j in range(1, group):
            for u, unit in enumerate(units):
                if unit[:2] == (step, 0):
                    lo_copy(u, part, group - j).wait_recv()
            total = total + lo_recv[step, part, j - 1].astype(jnp.float32)
        return total

    def hi_copy(step, part, slot, peer):
        return pltpu.make_async_remote_copy(
            src_ref=hi_send.at[step, part],
            dst_ref=hi_recv.at[slot, part],
            send_sem=hi_send_sem.at[step, part],
            recv_sem=hi_recv_sem.at[slot, part],
            device_id=(row, peer * group + place),
            device_id_type=MESH,
        )

    def hear(slot, part):
        hi_copy(0, part, slot, home).wait_recv()
        return hi_recv[slot, part].astype(jnp.float32)

    def send_on(step, *parts):
        for part in parts:
            total = near_sum(step, part)
            if step == 0:
                hi_send[step, part] = total.astype(jnp.bfloat16)
            else:

                @pl.when(inner)
                def _():
                    if (step, part) == (1, 0):
                        pl.semaphore_wait(relay_sem, 1)
                    hi_send[step, part] = (total + hear(step - 1, part)).astype(jnp.bfloat16)

                @pl.when(jnp.logical_not(inner))
                def _():
                    hi_send[step, part] = total.astype(jnp.bfloat16)

            slot = jnp.where(inner, STEPS - 1, step) if step == STEPS - 2 else step
            copy = hi_copy(step, part, slot, hi_peers[step])
            copy.start()
            hi_copies.append(copy)

    def finish(*parts):
        first_slot = jnp.where(inner, 2, 0)
        for part in parts:
            cols = slice(part * span * width, (part + 1) * span * width)
            total = near_sum(STEPS - 1, part) + hear(first_slot, part)
            out_ref[:, cols] = total + hear(first_slot + 1, part)

    small_copies[0].wait()
    pack_step(0)
    pl.semaphore_wait(barrier, len(greeted) + jnp.where(inner, 2, 1))
    first = len(units) - len(ORDER)
    send(*range(first))

    @pl.when(inner)
    def _():
        other = STEPS - 1 - home
        pl.semaphore_signal(relay_sem, inc=1, device_id=(row, other * group + place), device_id_type=MESH)

    send_twin(0)
    pack_step(1)
    send(first, first + 1)
    send_twin(1)
    pack_own(0)
    make_sums()
    for u in range(first):
        multiply(u)
    pack_step(2)
    send(first + 2, first + 3)
    send_twin(2)
    pack_step(3)
    send(first + 4, first + 5, first + 6)
    send_twin(3)
    pack_own(1)
    multiply(first)
    multiply(first + 1)
    pack_own(2)
    pack_own(3)
    send_on(0, 0, 1, 2, 3)
    multiply(first + 2)
    multiply(first + 3)
    send_on(1, 0, 1)
    multiply(first + 4, ((0, 1, 2), (2, 1, 3),))
    multiply(first + 5)
    send_on(2, 0, 1, 2, 3)
    multiply(first + 6)
    finish(0, 1, 2, 3)
    for copies in [x_copies, lo_copies, hi_copies]:
        for copy in copies:
            copy.wait_send()


def body(n_row, n_col, resid_tiles, tile_rows, tile_owner, tile_count, block_pick, basis):
    tiles = resid_tiles.reshape(resid_tiles.shape[1:])
    num_tiles, width, _ = tiles.shape
    rank = basis.shape[1]
    local_blocks = basis.reshape(-1, width, rank)
    held = local_blocks.shape[0]
    lanes = rank // STEPS
    group = n_col // STEPS
    piece = rank // n_col
    columns = RB_DEV * width
    part = columns // PARTS
    pairs = RB_DEV * n_row
    num_units = len(units_of(piece))
    hbm = pl.BlockSpec(memory_space=pl.ANY)
    dma = pltpu.SemaphoreType.DMA
    return pl.pallas_call(
        functools.partial(kernel, n_row, n_col),
        out_shape=pltpu.VMEM((piece, columns), jnp.float32),
        in_specs=[hbm] * 6,
        out_specs=pl.BlockSpec(memory_space=pltpu.VMEM),
        scratch_shapes=[
            pltpu.SMEM((1, num_tiles), jnp.int32),
            pltpu.SMEM((1, num_tiles), jnp.int32),
            pltpu.SMEM((1, 1), jnp.int32),
            pltpu.SMEM((1, n_row), jnp.int32),
            pltpu.VMEM((num_tiles, width, width), jnp.bfloat16),
            *[pltpu.VMEM((held, width, lanes), jnp.float32)] * STEPS,
            pltpu.VMEM((STEPS, n_row, group, piece, width), jnp.bfloat16),
            pltpu.VMEM((STEPS, n_row, group, piece, width), jnp.bfloat16),
            pltpu.VMEM((num_tiles + 1, width, width), jnp.float32),
            pltpu.VMEM((pairs, width, width), jnp.bfloat16),
            pltpu.VMEM((STEPS, PARTS, piece, part), jnp.float32),
            pltpu.VMEM((STEPS, PARTS, group - 1, piece, part), jnp.bfloat16),
            pltpu.VMEM((STEPS, PARTS, group - 1, piece, part), jnp.bfloat16),
            pltpu.VMEM((STEPS - 1, PARTS, piece, part), jnp.bfloat16),
            pltpu.VMEM((STEPS, PARTS, piece, part), jnp.bfloat16),
            pltpu.SMEM((num_tiles,), jnp.int32),
            pltpu.SMEM((pairs,), jnp.int32),
            dma((4,)),
            pltpu.SemaphoreType.REGULAR,
            dma,
            dma((STEPS,)),
            dma((num_units, n_row)),
            dma((num_units, n_row)),
            dma((STEPS,)),
            dma((STEPS,)),
            dma((num_units, PARTS, group - 1)),
            dma((num_units, PARTS, group - 1)),
            dma((STEPS - 1, PARTS)),
            dma((STEPS, PARTS)),
        ],
        compiler_params=pltpu.CompilerParams(
            collective_id=0, has_side_effects=True, vmem_limit_bytes=63 << 20
        ),
    )(tile_rows, tile_owner, tile_count, block_pick.reshape(1, n_row), tiles, local_blocks)


def solution(mesh):
    in_specs = (
        P("row", "col", None, None),
        P("row", "col"),
        P("row", "col"),
        P("row", "col"),
        P(None, "col", "row"),
        P(("col", "row"), None),
    )
    return jax.shard_map(
        functools.partial(body, mesh.shape["row"], mesh.shape["col"]),
        mesh=mesh,
        in_specs=in_specs,
        out_specs=P("col", "row"),
        check_vma=False,
    )
```

```python
import functools

import jax
import jax.numpy as jnp
from jax import lax
from jax.experimental import pallas as pl
from jax.experimental.pallas import tpu as pltpu
from jax.sharding import PartitionSpec as P

RB_DEV = 4
STEPS = 4
PARTS = 4
ORDER = ((1, 0), (0, 1), (2, 0), (1, 1), (3, 0), (2, 1), (3, 1))
MESH = pl.DeviceIdType.MESH


def flip(index):
    return index + 1 - 2 * lax.rem(index, 2)


def is_inner(home):
    return (home > 0) & (home < STEPS - 1)


def targets(home):
    inner = is_inner(home)
    far = jnp.where(home < STEPS // 2, STEPS - 1, 0)
    return [
        jnp.where(inner, STEPS - 1 - far, far),
        jnp.where(inner, far, lax.rem(home + 2, STEPS)),
        jnp.where(inner, STEPS - 1 - home, flip(home)),
        home,
    ]


def receivers(home):
    return [jnp.where(is_inner(home), target, flip(home)) for target in targets(home)[:-1]]


def units_of(piece):
    cut = 16 if piece > 16 else piece
    units = [(0, 0, 0, cut)]
    if cut < piece:
        units.append((0, 0, cut, piece - cut))
    units += [(step, side, 0, piece) for step, side in ORDER]
    return units


def kernel(
    n_row,
    n_col,
    rows_hbm,
    owners_hbm,
    count_hbm,
    picks_hbm,
    tiles_hbm,
    basis_hbm,
    out_ref,
    rows_s,
    owners_s,
    count_s,
    picks_s,
    tiles_v,
    basis_v0,
    basis_v1,
    basis_v2,
    basis_v3,
    x_send,
    x_recv,
    runs,
    sums,
    own,
    lo_send,
    lo_recv,
    hi_send,
    hi_recv,
    prev_s,
    last_s,
    small_sem,
    relay_sem,
    tiles_sem,
    basis_sem,
    x_send_sem,
    x_recv_sem,
    twin_send_sem,
    twin_recv_sem,
    lo_send_sem,
    lo_recv_sem,
    hi_send_sem,
    hi_recv_sem,
):
    basis_v = (basis_v0, basis_v1, basis_v2, basis_v3)
    num_tiles, width, _ = tiles_v.shape
    lanes = basis_v0.shape[2]
    group = n_col // STEPS
    piece = lanes // group
    pairs = RB_DEV * n_row
    span = RB_DEV // PARTS
    row = lax.axis_index("row")
    col = lax.axis_index("col")
    home = col // group
    place = lax.rem(col, group)
    inner = is_inner(home)

    chunks = targets(home)
    units = units_of(piece)
    hi_peers = receivers(home)
    twin_units = [[unit[0] for unit in units].index(step) for step in range(STEPS)]
    row_peers = []
    for j in range(n_row // 2 - 1, 0, -1):
        peer = lax.rem(row - lax.rem(row, 2) + 2 * j, n_row)
        row_peers += [peer, peer + 1]
    twin = flip(row)
    row_peers.append(twin)

    small_copies = []
    for n, (src, dst) in enumerate(
        [(picks_hbm, picks_s), (rows_hbm, rows_s), (owners_hbm, owners_s), (count_hbm, count_s)]
    ):
        copy = pltpu.make_async_copy(src, dst, small_sem.at[n])
        copy.start()
        small_copies.append(copy)
    basis_copies = []
    for step in range(STEPS):
        cols = pl.ds(pl.multiple_of(chunks[step] * lanes, lanes), lanes)
        copy = pltpu.make_async_copy(basis_hbm.at[:, :, cols], basis_v[step], basis_sem.at[step])
        copy.start()
        basis_copies.append(copy)
    tiles_copy = pltpu.make_async_copy(tiles_hbm, tiles_v, tiles_sem)
    tiles_copy.start()

    barrier = pltpu.get_barrier_semaphore()
    lo_peers = [lax.rem(place + j, group) for j in range(group)]
    greeted = [(peer, col) for peer in row_peers]
    greeted += [(row, home * group + peer) for peer in lo_peers[1:]]
    for peer in greeted:
        pl.semaphore_signal(barrier, inc=1, device_id=peer, device_id_type=MESH)

    @pl.when(home > 0)
    def _():
        pl.semaphore_signal(barrier, inc=1, device_id=(row, col - group), device_id_type=MESH)

    @pl.when(home < STEPS - 1)
    def _():
        pl.semaphore_signal(barrier, inc=1, device_id=(row, col + group), device_id_type=MESH)

    def pack(step, peer, ref):
        block = jnp.transpose(basis_v[step][picks_s[0, peer]]).astype(jnp.bfloat16)
        block = block.reshape(group, piece, width)
        for q in range(group):
            slot = lax.rem(q - place + group, group)
            ref[slot] = block[q]

    x_copies = []

    def x_copy(u, peer, sender):
        step, side, low, rows = units[u]
        slots = pl.ds(1, group - 1) if side == 0 else pl.ds(0, 1)
        return pltpu.make_async_remote_copy(
            src_ref=x_send.at[step, peer, slots, pl.ds(low, rows)],
            dst_ref=x_recv.at[step, sender, slots, pl.ds(low, rows)],
            send_sem=x_send_sem.at[u, peer],
            recv_sem=x_recv_sem.at[u, sender],
            device_id=(peer, col),
            device_id_type=MESH,
        )

    def twin_copy(step, sender):
        return pltpu.make_async_remote_copy(
            src_ref=x_send.at[step, twin],
            dst_ref=x_recv.at[step, sender],
            send_sem=twin_send_sem.at[step],
            recv_sem=twin_recv_sem.at[step],
            device_id=(twin, col),
            device_id_type=MESH,
        )

    def send_twin(*steps):
        for step in steps:
            copy = twin_copy(step, row)
            copy.start()
            x_copies.append(copy)

    def send(*us):
        for u in us:
            for peer in row_peers[:-1]:
                copy = x_copy(u, peer, row)
                copy.start()
                x_copies.append(copy)

    def pack_step(step):
        basis_copies[step].wait()
        for peer in row_peers:
            pack(step, peer, x_send.at[step, peer])

    def pack_own(step):
        pack(step, row, x_recv.at[step, row])

    def link(t, last):
        key = jnp.where(t < count_s[0, 0], rows_s[0, t] * n_row + owners_s[0, t], pairs)
        before = jnp.int32(num_tiles)
        new = []
        for p in range(pairs):
            before = jnp.where(key == p, last[p], before)
            new.append(jnp.where(key == p, t, last[p]))
        prev_s[t] = before
        return tuple(new)

    def run(t, carry):
        runs[t] = tiles_v[t].astype(jnp.float32) + runs[prev_s[t]]
        return carry

    def make_sums():
        for copy in small_copies[1:]:
            copy.wait()
        runs[num_tiles] = jnp.zeros((width, width), jnp.float32)
        last = (jnp.int32(num_tiles),) * pairs
        for t in range(num_tiles):
            last = link(t, last)
        for p in range(pairs):
            last_s[p] = last[p]
        tiles_copy.wait()
        lax.fori_loop(0, num_tiles, run, 0)
        for p in range(pairs):
            sums[p] = jnp.transpose(runs[last_s[p]].astype(jnp.bfloat16))

    lo_copies = []
    hi_copies = []

    def lo_copy(u, part, j):
        step, _, low, rows = units[u]
        rows = pl.ds(low, rows)
        return pltpu.make_async_remote_copy(
            src_ref=lo_send.at[step, part, j - 1, rows],
            dst_ref=lo_recv.at[step, part, group - j - 1, rows],
            send_sem=lo_send_sem.at[u, part, j - 1],
            recv_sem=lo_recv_sem.at[u, part, group - j - 1],
            device_id=(row, home * group + lo_peers[j]),
            device_id_type=MESH,
        )

    def product(u, part):
        step, side, low, rows = units[u]
        slots = range(1, group) if side == 0 else range(1)
        left = jnp.concatenate(
            [
                jnp.concatenate([x_recv[step, o, slot, low : low + rows] for slot in slots], axis=0)
                for o in range(n_row)
            ],
            axis=1,
        )
        out = []
        for i in range(part * span, (part + 1) * span):
            right = sums[i * n_row : (i + 1) * n_row].reshape(n_row * width, width)
            out.append(jnp.dot(left, right, preferred_element_type=jnp.float32))
        return jnp.concatenate(out, axis=1)

    def multiply(u, between=()):
        step, side, low, rows = units[u]
        if u in twin_units:
            twin_copy(step, twin).wait_recv()
        for peer in row_peers[:-1]:
            x_copy(u, peer, peer).wait_recv()
        for part in range(PARTS):
            total = product(u, part)
            if side:
                own[step, part, low : low + rows] = total
            else:
                total = total.astype(jnp.bfloat16)
                for j in range(1, group):
                    lo_send[step, part, j - 1, low : low + rows] = total[(j - 1) * rows : j * rows]
                    copy = lo_copy(u, part, j)
                    copy.start()
                    lo_copies.append(copy)
            for after, late_step, late_part in between:
                if after == part:
                    send_on(late_step, late_part)

    def near_sum(step, part):
        total = own[step, part]
        for j in range(1, group):
            for u, unit in enumerate(units):
                if unit[:2] == (step, 0):
                    lo_copy(u, part, group - j).wait_recv()
            total = total + lo_recv[step, part, j - 1].astype(jnp.float32)
        return total

    def hi_copy(step, part, slot, peer):
        return pltpu.make_async_remote_copy(
            src_ref=hi_send.at[step, part],
            dst_ref=hi_recv.at[slot, part],
            send_sem=hi_send_sem.at[step, part],
            recv_sem=hi_recv_sem.at[slot, part],
            device_id=(row, peer * group + place),
            device_id_type=MESH,
        )

    def hear(slot, part):
        hi_copy(0, part, slot, home).wait_recv()
        return hi_recv[slot, part].astype(jnp.float32)

    def send_on(step, *parts):
        for part in parts:
            total = near_sum(step, part)
            if step == 0:
                hi_send[step, part] = total.astype(jnp.bfloat16)
            else:

                @pl.when(inner)
                def _():
                    if (step, part) == (1, 0):
                        pl.semaphore_wait(relay_sem, 1)
                    hi_send[step, part] = (total + hear(step - 1, part)).astype(jnp.bfloat16)

                @pl.when(jnp.logical_not(inner))
                def _():
                    hi_send[step, part] = total.astype(jnp.bfloat16)

            slot = jnp.where(inner, STEPS - 1, step) if step == STEPS - 2 else step
            copy = hi_copy(step, part, slot, hi_peers[step])
            copy.start()
            hi_copies.append(copy)

    def finish(*parts):
        first_slot = jnp.where(inner, 2, 0)
        for part in parts:
            cols = slice(part * span * width, (part + 1) * span * width)
            total = near_sum(STEPS - 1, part) + hear(first_slot, part)
            out_ref[:, cols] = total + hear(first_slot + 1, part)

    small_copies[0].wait()
    pack_step(0)
    pl.semaphore_wait(barrier, len(greeted) + jnp.where(inner, 2, 1))
    first = len(units) - len(ORDER)
    send(*range(first))

    @pl.when(inner)
    def _():
        other = STEPS - 1 - home
        pl.semaphore_signal(relay_sem, inc=1, device_id=(row, other * group + place), device_id_type=MESH)

    send_twin(0)
    pack_step(1)
    send(first, first + 1)
    send_twin(1)
    pack_own(0)
    make_sums()
    for u in range(first):
        multiply(u)
    pack_step(2)
    send(first + 2, first + 3)
    send_twin(2)
    pack_step(3)
    send(first + 4, first + 5, first + 6)
    send_twin(3)
    pack_own(1)
    multiply(first)
    multiply(first + 1)
    pack_own(2)
    pack_own(3)
    send_on(0, 0, 1)
    multiply(first + 2, ((0, 0, 2), (1, 0, 3),))
    multiply(first + 3)
    send_on(1, 0, 1)
    multiply(first + 4, ((1, 1, 2), (3, 1, 3),))
    multiply(first + 5, ((1, 2, 0), (3, 2, 1),))
    send_on(2, 2, 3)
    multiply(first + 6)
    finish(0, 1, 2, 3)
    for copies in [x_copies, lo_copies, hi_copies]:
        for copy in copies:
            copy.wait_send()


def body(n_row, n_col, resid_tiles, tile_rows, tile_owner, tile_count, block_pick, basis):
    tiles = resid_tiles.reshape(resid_tiles.shape[1:])
    num_tiles, width, _ = tiles.shape
    rank = basis.shape[1]
    local_blocks = basis.reshape(-1, width, rank)
    held = local_blocks.shape[0]
    lanes = rank // STEPS
    group = n_col // STEPS
    piece = rank // n_col
    columns = RB_DEV * width
    part = columns // PARTS
    pairs = RB_DEV * n_row
    num_units = len(units_of(piece))
    hbm = pl.BlockSpec(memory_space=pl.ANY)
    dma = pltpu.SemaphoreType.DMA
    return pl.pallas_call(
        functools.partial(kernel, n_row, n_col),
        out_shape=pltpu.VMEM((piece, columns), jnp.float32),
        in_specs=[hbm] * 6,
        out_specs=pl.BlockSpec(memory_space=pltpu.VMEM),
        scratch_shapes=[
            pltpu.SMEM((1, num_tiles), jnp.int32),
            pltpu.SMEM((1, num_tiles), jnp.int32),
            pltpu.SMEM((1, 1), jnp.int32),
            pltpu.SMEM((1, n_row), jnp.int32),
            pltpu.VMEM((num_tiles, width, width), jnp.bfloat16),
            *[pltpu.VMEM((held, width, lanes), jnp.float32)] * STEPS,
            pltpu.VMEM((STEPS, n_row, group, piece, width), jnp.bfloat16),
            pltpu.VMEM((STEPS, n_row, group, piece, width), jnp.bfloat16),
            pltpu.VMEM((num_tiles + 1, width, width), jnp.float32),
            pltpu.VMEM((pairs, width, width), jnp.bfloat16),
            pltpu.VMEM((STEPS, PARTS, piece, part), jnp.float32),
            pltpu.VMEM((STEPS, PARTS, group - 1, piece, part), jnp.bfloat16),
            pltpu.VMEM((STEPS, PARTS, group - 1, piece, part), jnp.bfloat16),
            pltpu.VMEM((STEPS - 1, PARTS, piece, part), jnp.bfloat16),
            pltpu.VMEM((STEPS, PARTS, piece, part), jnp.bfloat16),
            pltpu.SMEM((num_tiles,), jnp.int32),
            pltpu.SMEM((pairs,), jnp.int32),
            dma((4,)),
            pltpu.SemaphoreType.REGULAR,
            dma,
            dma((STEPS,)),
            dma((num_units, n_row)),
            dma((num_units, n_row)),
            dma((STEPS,)),
            dma((STEPS,)),
            dma((num_units, PARTS, group - 1)),
            dma((num_units, PARTS, group - 1)),
            dma((STEPS - 1, PARTS)),
            dma((STEPS, PARTS)),
        ],
        compiler_params=pltpu.CompilerParams(
            collective_id=0, has_side_effects=True, vmem_limit_bytes=63 << 20
        ),
    )(tile_rows, tile_owner, tile_count, block_pick.reshape(1, n_row), tiles, local_blocks)


def solution(mesh):
    in_specs = (
        P("row", "col", None, None),
        P("row", "col"),
        P("row", "col"),
        P("row", "col"),
        P(None, "col", "row"),
        P(("col", "row"), None),
    )
    return jax.shard_map(
        functools.partial(body, mesh.shape["row"], mesh.shape["col"]),
        mesh=mesh,
        in_specs=in_specs,
        out_specs=P("col", "row"),
        check_vma=False,
    )
```
